32 devices in a mesh: groups: 2 (over x), ctx: 16 (over z, y, core).
Axes of the slice: x: 2, y: 2, z: 4, core: 2. Of those that a mesh axis runs over, the one named last changes fastest.
Arguments:
- queries: bfloat16 [64, 8192], P(('groups', 'ctx')), parts along dimension 0, may hold values from -256 to 256, as said below
- cached_key_rows: bfloat16 [16384, 1024], P(('groups', 'ctx')), parts along dimension 0, may hold values from -4 to 4, as said below
- cached_value_rows: bfloat16 [16384, 1024], P(('groups', 'ctx')), parts along dimension 0, may hold values from -6 to 6
- cache_position: int32 [16384], P(('groups', 'ctx')), parts along dimension 0, may hold values from 0 to 8191, as said below
- lengths: int32 [64], P(('groups', 'ctx')), parts along dimension 0, may hold values from 2 to 8192, as said below
- norm_gain: float32 [8192], replicated, may hold values from 0.5 to 1.5
- gate_weight: bfloat16 [14336, 8192], P('ctx'), may hold values from -0.0625 to 0.0625
- up_weight: bfloat16 [14336, 8192], P('ctx'), may hold values from -0.0625 to 0.0625
- down_weight: bfloat16 [14336, 8192], P('ctx'), may hold values from -0.046875 to 0.046875
Outputs:
- layer_out: bfloat16 [64, 8192], P(('groups', 'ctx')), parts along dimension 0
The draws below stay inside these ranges and needn't reach their ends.
There are 2 independent parts, one for each index of `groups`. The reference program is written for one: setup_inputs(seed, part) draws one part's arguments, and reference() takes and returns one part's arrays. A program takes and returns all parts, laid end to end along the dimension named above; an argument that names none is the same for every part. Nothing has to cross between parts.
Inputs may be any that keep to these rules, and one draw needn't show every extreme that they name: `queries`: queries stay within the stated range. `cached_key_rows`: keys stay within the stated range. `cache_position`: A permutation of 0 to 8191. `lengths`: some row has length 8192 and some row has length 2.
All inputs are finite; a program needn't handle non-finite values.
Results may differ from the reference program's by a relative error of at most 0.02.
Values may be sent and summed in bfloat16 or wider, within the bound.
No kernel may reach another device: no remote copies, remote signals or barrier semaphores. Data moves between devices by JAX's collectives and lax.ppermute only.
A program may use at most 128 MiB of HBM per device.

```python
import jax
import jax.numpy as jnp
from jax import lax

D = 8192
QUERY_HEADS = 64
KEY_VALUE_HEADS = 8
HEAD_SIZE = 128
FFH = 14336
ROWS = 32
CACHE_SLOTS = 8192


def cache_order(key):
    return jax.random.permutation(jax.random.fold_in(key, 11), CACHE_SLOTS).astype(jnp.int32)


def random_base_keys(key):
    sampled_entries = jax.random.normal(jax.random.fold_in(key, 23), (CACHE_SLOTS, KEY_VALUE_HEADS * HEAD_SIZE), jnp.float32)
    return jnp.clip(sampled_entries, -4.0, 4.0)


def draw_cache_position(key, part):
    return cache_order(key)


def draw_cached_key_rows(key, part):
    keyed = random_base_keys(key)
    return keyed.astype(jnp.bfloat16)


def draw_queries(key, part):
    sampled_entries = jax.random.normal(jax.random.fold_in(key, 31), (ROWS, QUERY_HEADS * HEAD_SIZE), jnp.float32)
    sampled_entries = jnp.clip(sampled_entries, -4.0, 4.0)
    return sampled_entries.astype(jnp.bfloat16)


def draw_lengths(key, part):
    sampled_entries = jax.random.randint(jax.random.fold_in(key, 53), (ROWS,), 2, CACHE_SLOTS + 1).astype(jnp.int32)
    first_row = jax.random.randint(jax.random.fold_in(key, 59), (), 0, ROWS).astype(jnp.int32)
    offset_row = jax.random.randint(jax.random.fold_in(key, 61), (), 0, ROWS - 1).astype(jnp.int32)
    second_row = (first_row + 1 + offset_row) % ROWS
    sampled_entries = sampled_entries.at[first_row].set(CACHE_SLOTS)
    sampled_entries = sampled_entries.at[second_row].set(2)
    return sampled_entries


def level_of(rng, extent, split, low, high):
    gain, own = 1.0, jax.random.fold_in(rng, 6)
    for position, parts in split:
        steps = jnp.exp(jax.random.uniform(jax.random.fold_in(own, position), (parts,), jnp.float32, low / len(split), high / len(split)))
        gain = gain * jnp.repeat(steps, extent[position] // parts).reshape([-1 if axis == position else 1 for axis in range(len(extent))])
    return gain


def scatter_about(rng, shape, scale, bound, cuts=(), held_as=jnp.bfloat16):
    values = jax.random.normal(rng, shape, jnp.float32) * scale
    if len(cuts) > 0:
        values = level_of(rng, shape, cuts, -0.22, 0.18) * values
    return jnp.clip(values, min=-bound, max=bound).astype(held_as)


def setup_inputs(seed: int = 0, part: int = 0) -> dict:
    key_of = jax.random.split(jax.random.key(seed), 10)
    part_keys = jax.random.split(jax.random.fold_in(key_of[9], part), 10)
    queries = draw_queries(jax.random.fold_in(jax.random.fold_in(key_of[9], part), 71), part)
    cached_key_rows = draw_cached_key_rows(jax.random.fold_in(jax.random.fold_in(key_of[9], part), 71), part)
    cached_value_rows = scatter_about(part_keys[2], (CACHE_SLOTS, KEY_VALUE_HEADS * HEAD_SIZE), 1.0, 6.0, ((0, 16),))
    cache_position = draw_cache_position(jax.random.fold_in(jax.random.fold_in(key_of[9], part), 71), part)
    lengths = draw_lengths(jax.random.fold_in(jax.random.fold_in(key_of[9], part), 71), part)
    norm_gain = jnp.clip(jax.random.uniform(key_of[5], (D,), jnp.float32, 0.5, 1.5), 0.5, 1.5)
    gate_weight = scatter_about(key_of[6], (FFH, D), D ** -0.5, 0.0625, ((0, 16),))
    up_weight = scatter_about(key_of[7], (FFH, D), D ** -0.5, 0.0625, ((0, 16),))
    down_weight = scatter_about(key_of[8], (FFH, D), FFH ** -0.5, 0.046875, ((0, 16),))
    return {"queries": queries, "cached_key_rows": cached_key_rows, "cached_value_rows": cached_value_rows, "cache_position": cache_position, "lengths": lengths, "norm_gain": norm_gain, "gate_weight": gate_weight, "up_weight": up_weight, "down_weight": down_weight}


def reference(queries, cached_key_rows, cached_value_rows, cache_position, lengths, norm_gain, gate_weight, up_weight, down_weight):
    query_group_size = QUERY_HEADS // KEY_VALUE_HEADS
    key_head_count = cached_key_rows.astype(jnp.float32).reshape(CACHE_SLOTS, KEY_VALUE_HEADS, HEAD_SIZE)
    value_head_count = cached_value_rows.astype(jnp.float32).reshape(CACHE_SLOTS, KEY_VALUE_HEADS, HEAD_SIZE)
    count_of_blocks = ROWS // 8
    query_block_list = queries.astype(jnp.float32).reshape(count_of_blocks, 8, KEY_VALUE_HEADS, query_group_size, HEAD_SIZE)
    length_blocks = lengths.reshape(count_of_blocks, 8)

    def attend(pieces):
        query_block, length_block = pieces
        scores = jnp.einsum('rkgd,tkd->rkgt', query_block, key_head_count) * HEAD_SIZE ** (-0.5)
        live = (cache_position[None, :] < length_block[:, None])[:, None, None, :]
        scores = jnp.where(live, scores, -1e+30)
        peak = lax.optimization_barrier(jnp.max(scores, axis=3, keepdims=True))
        weights = jnp.where(live, jnp.exp(scores - peak), 0.0)
        totals = lax.optimization_barrier(jnp.sum(weights, axis=3))
        rounded = lax.optimization_barrier(weights.astype(jnp.bfloat16)).astype(jnp.float32)
        summed = jnp.einsum('rkgt,tkd->rkgd', rounded, value_head_count)
        return (summed / totals[..., None]).reshape(8, D)
    attended = lax.map(attend, (query_block_list, length_blocks)).reshape(ROWS, D).astype(jnp.bfloat16)
    widened = attended.astype(jnp.float32)
    mean_square = lax.optimization_barrier(jnp.mean(widened * widened, axis=1, keepdims=True)) + 1e-05
    normed = (widened * lax.rsqrt(mean_square) * norm_gain[None, :]).astype(jnp.bfloat16)
    gate = jnp.dot(normed, gate_weight.T, preferred_element_type=jnp.float32)
    upward = jnp.dot(normed, up_weight.T, preferred_element_type=jnp.float32)
    activated = (jax.nn.silu(gate) * upward).astype(jnp.bfloat16)
    return jnp.dot(activated, down_weight, preferred_element_type=jnp.float32).astype(jnp.bfloat16)
```

```python
import functools

import jax
import jax.numpy as jnp
from jax import lax
from jax.experimental import pallas as pl
from jax.experimental.pallas import tpu as pltpu
from jax.sharding import PartitionSpec as P

D = 8192
QUERY_HEADS = 64
KEY_VALUE_HEADS = 8
HEAD_SIZE = 128
GROUP = QUERY_HEADS // KEY_VALUE_HEADS
F32 = jnp.float32
BF16 = jnp.bfloat16
ROWS_BY_ROWS = (((1,), (1,)), ((), ()))
VMEM = pl.BlockSpec(memory_space=pltpu.VMEM)
SMEM = pl.BlockSpec(memory_space=pltpu.SMEM)
ANY = pl.BlockSpec(memory_space=pl.ANY)
MIB = 1 << 20


def in_vmem(x):
    return pltpu.with_memory_space_constraint(x, pltpu.VMEM)


def rounded(x):
    return x.astype(BF16).astype(F32)


def pack_kernel(lengths_ref, q_ref, out_ref, slab_ref):
    rows = q_ref.shape[0]
    q = q_ref[...].astype(F32)
    lane = lax.broadcasted_iota(jnp.int32, (GROUP, HEAD_SIZE), 1)
    for row in range(rows):
        for head in range(QUERY_HEADS):
            slot = row * GROUP + head % GROUP
            slab_ref[head // GROUP, slot : slot + 1, :] = q[
                row : row + 1, head * HEAD_SIZE : (head + 1) * HEAD_SIZE
            ]
        length = lengths_ref[row]
        high, low = (length >> 8).astype(F32), (length & 255).astype(F32)
        slab_ref[KEY_VALUE_HEADS, row * GROUP : (row + 1) * GROUP, :] = jnp.where(
            lane == 0, high, jnp.where(lane == 1, low, 0.0)
        )
    packed = slab_ref[...].astype(BF16)
    for peer in range(out_ref.shape[0]):
        out_ref[peer] = packed


def pack(queries, lengths, peers):
    slots = queries.shape[0] * GROUP
    shape = (KEY_VALUE_HEADS + 1, slots, HEAD_SIZE)
    return pl.pallas_call(
        pack_kernel,
        out_shape=pltpu.VMEM((peers,) + shape, BF16),
        in_specs=[SMEM, VMEM],
        out_specs=VMEM,
        scratch_shapes=[pltpu.VMEM(shape, F32)],
        compiler_params=pltpu.CompilerParams(vmem_limit_bytes=4 * MIB),
        name="pack",
    )(lengths, queries)


def attend_kernel(
    near_ref, far_ref, position_ref, k_hbm, v_hbm, w_hbm,
    keep_ref, send_ref, w_ref, k_ref, v_ref, sems,
):
    copies = [
        pltpu.make_async_copy(source, target, sems.at[i])
        for i, (source, target) in enumerate(((k_hbm, k_ref), (v_hbm, v_ref), (w_hbm, w_ref)))
    ]
    for copy in copies:
        copy.start()
    peers, _, slots, _ = near_ref.shape
    half = peers * slots

    def slab(g):
        return jnp.concatenate(
            [ref[:, g].reshape(half, HEAD_SIZE) for ref in (near_ref, far_ref)], axis=0
        )

    numbers = slab(KEY_VALUE_HEADS).astype(F32)
    lengths = numbers[:, 0:1] * 256.0 + numbers[:, 1:2]
    live = position_ref[...].astype(F32) < lengths
    lane = lax.broadcasted_iota(jnp.int32, (2 * half, HEAD_SIZE), 1)
    state = jnp.zeros((2 * half, HEAD_SIZE), F32)
    copies[0].wait()
    copies[1].wait()
    for g in range(KEY_VALUE_HEADS):
        columns = slice(g * HEAD_SIZE, (g + 1) * HEAD_SIZE)
        scores = lax.dot_general(
            slab(g), k_ref[:, columns], ROWS_BY_ROWS, preferred_element_type=F32
        ) * HEAD_SIZE ** (-0.5)
        scores = jnp.where(live, scores, -1e30)
        peak = rounded(jnp.max(scores, axis=1, keepdims=True))
        weights = jnp.where(live, jnp.exp(scores - peak), 0.0)
        total = jnp.sum(weights, axis=1, keepdims=True)
        summed = jnp.dot(weights.astype(BF16), v_ref[:, columns], preferred_element_type=F32)
        total_high = rounded(total)
        for index, column in enumerate((peak, total_high, total - total_high)):
            state = jnp.where(lane == index * KEY_VALUE_HEADS + g, column, state)
        keep_ref[:, g] = summed[:half].reshape(peers, slots, HEAD_SIZE)
        send_ref[:, g] = summed[half:].astype(BF16).reshape(peers, slots, HEAD_SIZE)
    keep_ref[:, KEY_VALUE_HEADS] = state[:half].reshape(peers, slots, HEAD_SIZE)
    send_ref[:, KEY_VALUE_HEADS] = state[half:].astype(BF16).reshape(peers, slots, HEAD_SIZE)
    copies[2].wait()


def attend(near, far, position, keys, values, weight):
    cells = near.size // HEAD_SIZE * keys.shape[0]
    return pl.pallas_call(
        attend_kernel,
        out_shape=(
            pltpu.VMEM(near.shape, F32),
            pltpu.VMEM(near.shape, BF16),
            pltpu.VMEM(weight.shape, weight.dtype),
        ),
        in_specs=[VMEM, VMEM, VMEM, ANY, ANY, ANY],
        out_specs=(VMEM, VMEM, VMEM),
        scratch_shapes=[
            pltpu.VMEM(keys.shape, keys.dtype),
            pltpu.VMEM(values.shape, values.dtype),
            pltpu.SemaphoreType.DMA((3,)),
        ],
        compiler_params=pltpu.CompilerParams(vmem_limit_bytes=20 * MIB),
        cost_estimate=pl.CostEstimate(
            flops=8 * cells * HEAD_SIZE, bytes_accessed=2 * weight.size, transcendentals=2 * cells
        ),
        name="attend",
    )(in_vmem(near), in_vmem(far), position, keys, values, weight)


def state_columns(state, g):
    peak, high, low = (
        state[:, i * KEY_VALUE_HEADS + g : i * KEY_VALUE_HEADS + g + 1] for i in range(3)
    )
    return peak, high + low


def merge_kernel(keep_ref, came_ref, out_ref):
    peers, _, slots, _ = keep_ref.shape
    flat = (peers * slots, HEAD_SIZE)
    mine = keep_ref[:, KEY_VALUE_HEADS].reshape(flat)
    theirs = came_ref[:, KEY_VALUE_HEADS].astype(F32).reshape(flat)
    lane = lax.broadcasted_iota(jnp.int32, flat, 1)
    state = jnp.zeros(flat, F32)
    for g in range(KEY_VALUE_HEADS):
        my_peak, my_total = state_columns(mine, g)
        their_peak, their_total = state_columns(theirs, g)
        peak = jnp.maximum(my_peak, their_peak)
        my_scale, their_scale = jnp.exp(my_peak - peak), jnp.exp(their_peak - peak)
        total = my_total * my_scale + their_total * their_scale
        summed = (
            keep_ref[:, g].reshape(flat) * my_scale
            + came_ref[:, g].astype(F32).reshape(flat) * their_scale
        )
        total_high = rounded(total)
        for index, column in enumerate((peak, total_high, total - total_high)):
            state = jnp.where(lane == index * KEY_VALUE_HEADS + g, column, state)
        out_ref[:, g] = summed.astype(BF16).reshape(peers, slots, HEAD_SIZE)
    out_ref[:, KEY_VALUE_HEADS] = state.astype(BF16).reshape(peers, slots, HEAD_SIZE)


def merge(keep, came):
    return pl.pallas_call(
        merge_kernel,
        out_shape=pltpu.VMEM(came.shape, BF16),
        in_specs=[VMEM, VMEM],
        out_specs=VMEM,
        compiler_params=pltpu.CompilerParams(vmem_limit_bytes=8 * MIB),
        name="merge",
    )(in_vmem(keep), in_vmem(came))


def finish_kernel(parts_ref, gain_ref, out_ref, row_ref):
    peers, _, slots, _ = parts_ref.shape
    rows = slots // GROUP
    state = parts_ref[:, KEY_VALUE_HEADS].astype(F32)
    scale = jnp.exp(state - jnp.max(state, axis=0, keepdims=True))
    attended = []
    squares = jnp.zeros((slots, HEAD_SIZE), F32)
    for g in range(KEY_VALUE_HEADS):
        summed = jnp.zeros((slots, HEAD_SIZE), F32)
        total = jnp.zeros((slots, 1), F32)
        for peer in range(peers):
            by = scale[peer][:, g : g + 1]
            summed += parts_ref[peer, g].astype(F32) * by
            total += state_columns(state[peer], g)[1] * by
        one = rounded(summed / total)
        squares += one * one
        attended.append(one)
    mean_square = (
        jnp.sum(squares.reshape(rows, GROUP, HEAD_SIZE), axis=(1, 2), keepdims=True) / D + 1e-05
    )
    inverse = lax.rsqrt(mean_square)
    for g in range(KEY_VALUE_HEADS):
        normed = attended[g].reshape(rows, GROUP, HEAD_SIZE) * inverse * gain_ref[g][None]
        for row in range(rows):
            for head in range(GROUP):
                start = (g * GROUP + head) * HEAD_SIZE
                row_ref[row : row + 1, start : start + HEAD_SIZE] = normed[row, head : head + 1]
    packed = row_ref[...].astype(BF16)
    for peer in range(peers):
        out_ref[peer] = packed


def finish(parts, norm_gain):
    peers, _, slots, _ = parts.shape
    rows = slots // GROUP
    return pl.pallas_call(
        finish_kernel,
        out_shape=pltpu.VMEM((peers, rows, D), BF16),
        in_specs=[VMEM, VMEM],
        out_specs=VMEM,
        scratch_shapes=[pltpu.VMEM((rows, D), F32)],
        compiler_params=pltpu.CompilerParams(vmem_limit_bytes=8 * MIB),
        name="finish",
    )(in_vmem(parts), norm_gain.reshape(KEY_VALUE_HEADS, GROUP, HEAD_SIZE))


def feed_forward_kernel(
    near_ref, far_ref, gate_ref, up_hbm, down_hbm, keep_ref, send_ref, x_ref, up_ref, down_ref, sems,
    *, chunks,
):
    half, width = near_ref.shape
    step = width // chunks

    def copies(source, target, base):
        return [
            pltpu.make_async_copy(
                source.at[:, pl.ds(i * step, step)], target.at[:, pl.ds(i * step, step)], sems.at[base + i]
            )
            for i in range(chunks)
        ]

    ups, downs = copies(up_hbm, up_ref, 0), copies(down_hbm, down_ref, chunks)
    for copy in ups + downs:
        copy.start()
    x_ref[:half] = near_ref[...]
    x_ref[half:] = far_ref[...]
    hidden = gate_ref.shape[0]
    gate = lax.dot_general(x_ref[...], gate_ref[...], ROWS_BY_ROWS, preferred_element_type=F32)
    gate = gate / (1.0 + jnp.exp(-gate))
    upward = jnp.zeros((2 * half, hidden), F32)
    for i, copy in enumerate(ups):
        copy.wait()
        part = slice(i * step, (i + 1) * step)
        upward += lax.dot_general(
            x_ref[:, part], up_ref[:, part], ROWS_BY_ROWS, preferred_element_type=F32
        )
    activated = (gate * upward).astype(BF16)
    for i, copy in enumerate(downs):
        copy.wait()
        part = slice(i * step, (i + 1) * step)
        out = jnp.dot(activated, down_ref[:, part], preferred_element_type=F32)
        keep_ref[:, part] = out[:half]
        send_ref[:, part] = out[half:].astype(BF16)


def feed_forward(near, far, gate, up, down):
    half, width = near.shape
    chunks = 8
    return pl.pallas_call(
        functools.partial(feed_forward_kernel, chunks=chunks),
        out_shape=(pltpu.VMEM(near.shape, F32), pltpu.VMEM(near.shape, BF16)),
        in_specs=[VMEM, VMEM, VMEM, ANY, ANY],
        out_specs=(VMEM, VMEM),
        scratch_shapes=[
            pltpu.VMEM((2 * half, width), BF16),
            pltpu.VMEM(up.shape, up.dtype),
            pltpu.VMEM(down.shape, down.dtype),
            pltpu.SemaphoreType.DMA((2 * chunks,)),
        ],
        compiler_params=pltpu.CompilerParams(vmem_limit_bytes=40 * MIB),
        cost_estimate=pl.CostEstimate(
            flops=12 * half * gate.size, bytes_accessed=4 * up.size, transcendentals=half * up.shape[0]
        ),
        name="feed_forward",
    )(in_vmem(near), in_vmem(far), in_vmem(gate), up, down)


def stacked(blocks):
    peers, rows, _ = blocks.shape
    out = None
    for i in range(peers):
        edges = ((i * rows, (peers - 1 - i) * rows, 0), (0, 0, 0))
        placed = lax.pad(blocks[i], jnp.array(-jnp.inf, blocks.dtype), edges)
        out = placed if out is None else jnp.maximum(out, placed)
    return out


def local(
    queries,
    cached_key_rows,
    cached_value_rows,
    cache_position,
    lengths,
    norm_gain,
    gate_weight,
    up_weight,
    down_weight,
):
    devices = lax.axis_size("ctx")
    peers = devices // 2
    rows = queries.shape[0]
    same_core = [[2 * i + core for i in range(peers)] for core in range(2)]
    partners = [(i, i ^ 1) for i in range(devices)]

    def exchange(x):
        return lax.all_to_all(x, "ctx", 0, 0, axis_index_groups=same_core, tiled=True)

    def swap(x):
        return lax.ppermute(x, "ctx", partners)

    near = exchange(pack(queries, lengths, peers))
    keep, send, gate = attend(
        near, swap(near), cache_position.reshape(1, -1), cached_key_rows, cached_value_rows, gate_weight
    )
    parts = exchange(merge(keep, swap(send)))
    near = stacked(exchange(finish(parts, norm_gain)))
    keep, send = feed_forward(near, swap(near), gate, up_weight, down_weight)
    shares = (keep + swap(send).astype(F32)).astype(BF16)
    shares = exchange(shares.reshape(peers, rows, D))
    return jnp.sum(shares.astype(F32), axis=0).astype(BF16)


def solution(mesh):
    placed = (
        P(("groups", "ctx"), None),
        P(("groups", "ctx"), None),
        P(("groups", "ctx"), None),
        P(("groups", "ctx")),
        P(("groups", "ctx")),
        P(),
        P("ctx", None),
        P("ctx", None),
        P("ctx", None),
    )
    return jax.shard_map(
        local, mesh=mesh, in_specs=placed, out_specs=P(("groups", "ctx"), None), check_vma=False
    )
```

```python
import functools

import jax
import jax.numpy as jnp
from jax import lax
from jax.experimental import pallas as pl
from jax.experimental.pallas import tpu as pltpu
from jax.sharding import PartitionSpec as P

D = 8192
QUERY_HEADS = 64
KEY_VALUE_HEADS = 8
HEAD_SIZE = 128
GROUP = QUERY_HEADS // KEY_VALUE_HEADS
F32 = jnp.float32
BF16 = jnp.bfloat16
ROWS_BY_ROWS = (((1,), (1,)), ((), ()))
VMEM = pl.BlockSpec(memory_space=pltpu.VMEM)
ANY = pl.BlockSpec(memory_space=pl.ANY)
MIB = 1 << 20


def in_vmem(x):
    return pltpu.with_memory_space_constraint(x, pltpu.VMEM)


def in_hbm(x):
    return pltpu.with_memory_space_constraint(x, pltpu.HBM)


def rounded(x):
    return x.astype(BF16).astype(F32)


def pack_kernel(lengths_hbm, q_hbm, out_ref, slab_ref, lengths_ref, q_ref, sems):
    rows = q_ref.shape[0]
    copies = (
        pltpu.make_async_copy(q_hbm, q_ref, sems.at[0]),
        pltpu.make_async_copy(lengths_hbm, lengths_ref, sems.at[1]),
    )
    for copy in copies:
        copy.start()
    for copy in copies:
        copy.wait()
    q = q_ref[...].astype(F32)
    lane = lax.broadcasted_iota(jnp.int32, (GROUP, HEAD_SIZE), 1)
    for row in range(rows):
        for head in range(QUERY_HEADS):
            slot = row * GROUP + head % GROUP
            slab_ref[head // GROUP, slot : slot + 1, :] = q[
                row : row + 1, head * HEAD_SIZE : (head + 1) * HEAD_SIZE
            ]
        length = lengths_ref[row]
        high, low = (length >> 8).astype(F32), (length & 255).astype(F32)
        slab_ref[KEY_VALUE_HEADS, row * GROUP : (row + 1) * GROUP, :] = jnp.where(
            lane == 0, high, jnp.where(lane == 1, low, 0.0)
        )
    packed = slab_ref[...].astype(BF16)
    for peer in range(out_ref.shape[0]):
        out_ref[peer] = packed


def pack(queries, lengths, peers):
    slots = queries.shape[0] * GROUP
    shape = (KEY_VALUE_HEADS + 1, slots, HEAD_SIZE)
    return pl.pallas_call(
        pack_kernel,
        out_shape=pltpu.VMEM((peers,) + shape, BF16),
        in_specs=[ANY, ANY],
        out_specs=VMEM,
        scratch_shapes=[
            pltpu.VMEM(shape, F32),
            pltpu.SMEM(lengths.shape, lengths.dtype),
            pltpu.VMEM(queries.shape, queries.dtype),
            pltpu.SemaphoreType.DMA((2,)),
        ],
        compiler_params=pltpu.CompilerParams(vmem_limit_bytes=4 * MIB),
        name="pack",
    )(in_hbm(lengths), in_hbm(queries))


def load_kernel(*refs, starts):
    count = len(starts)
    copies = [
        pltpu.make_async_copy(
            refs[i].at[pl.ds(start, refs[count + i].shape[0])], refs[count + i], refs[-1].at[i]
        )
        for i, start in enumerate(starts)
    ]
    for copy in copies:
        copy.start()
    for copy in copies:
        copy.wait()


def load(*entries):
    shapes = [((a.shape[0] - start,) + a.shape[1:], a.dtype) for a, start in entries]
    return pl.pallas_call(
        functools.partial(load_kernel, starts=tuple(start for _, start in entries)),
        out_shape=tuple(pltpu.VMEM(*shape) for shape in shapes),
        in_specs=[ANY] * len(entries),
        out_specs=(VMEM,) * len(entries),
        scratch_shapes=[pltpu.SemaphoreType.DMA((len(entries),))],
        compiler_params=pltpu.CompilerParams(vmem_limit_bytes=MIB),
        cost_estimate=pl.CostEstimate(
            flops=0, bytes_accessed=sum(4 * a.size for a, _ in entries), transcendentals=0
        ),
        name="load",
    )(*(in_hbm(a) for a, _ in entries))


def attend_kernel(
    near_ref, far_ref, position_ref, k_ref, v_ref, w_hbm, keep_ref, send_ref, w_ref, sem
):
    copy = pltpu.make_async_copy(w_hbm.at[pl.ds(0, w_ref.shape[0])], w_ref, sem)
    copy.start()
    peers, _, slots, _ = near_ref.shape
    half = peers * slots

    def slab(g):
        return jnp.concatenate(
            [ref[:, g].reshape(half, HEAD_SIZE) for ref in (near_ref, far_ref)], axis=0
        )

    numbers = slab(KEY_VALUE_HEADS).astype(F32)
    lengths = numbers[:, 0:1] * 256.0 + numbers[:, 1:2]
    live = position_ref[...].astype(F32) < lengths
    lane = lax.broadcasted_iota(jnp.int32, (2 * half, HEAD_SIZE), 1)
    state = jnp.zeros((2 * half, HEAD_SIZE), F32)
    for g in range(KEY_VALUE_HEADS):
        columns = slice(g * HEAD_SIZE, (g + 1) * HEAD_SIZE)
        scores = lax.dot_general(
            slab(g), k_ref[:, columns], ROWS_BY_ROWS, preferred_element_type=F32
        ) * HEAD_SIZE ** (-0.5)
        scores = jnp.where(live, scores, -1e30)
        peak = rounded(jnp.max(scores, axis=1, keepdims=True))
        weights = jnp.where(live, jnp.exp(scores - peak), 0.0)
        total = jnp.sum(weights, axis=1, keepdims=True)
        summed = jnp.dot(weights.astype(BF16), v_ref[:, columns], preferred_element_type=F32)
        total_high = rounded(total)
        for index, column in enumerate((peak, total_high, total - total_high)):
            state = jnp.where(lane == index * KEY_VALUE_HEADS + g, column, state)
        keep_ref[:, g] = summed[:half].reshape(peers, slots, HEAD_SIZE)
        send_ref[:, g] = summed[half:].astype(BF16).reshape(peers, slots, HEAD_SIZE)
    keep_ref[:, KEY_VALUE_HEADS] = state[:half].reshape(peers, slots, HEAD_SIZE)
    send_ref[:, KEY_VALUE_HEADS] = state[half:].astype(BF16).reshape(peers, slots, HEAD_SIZE)
    copy.wait()


def attend(near, far, position, keys, values, weight, weight_rows):
    cells = near.size // HEAD_SIZE * keys.shape[0]
    return pl.pallas_call(
        attend_kernel,
        out_shape=(
            pltpu.VMEM(near.shape, F32),
            pltpu.VMEM(near.shape, BF16),
            pltpu.VMEM((weight_rows, weight.shape[1]), weight.dtype),
        ),
        in_specs=[VMEM] * 5 + [ANY],
        out_specs=(VMEM,) * 3,
        scratch_shapes=[pltpu.SemaphoreType.DMA],
        compiler_params=pltpu.CompilerParams(vmem_limit_bytes=12 * MIB + 16 * near.size),
        cost_estimate=pl.CostEstimate(
            flops=8 * cells * HEAD_SIZE, bytes_accessed=4 * keys.size, transcendentals=2 * cells
        ),
        name="attend",
    )(*(in_vmem(x) for x in (near, far, position, keys, values)), in_hbm(weight))


def state_columns(state, g):
    peak, high, low = (
        state[:, i * KEY_VALUE_HEADS + g : i * KEY_VALUE_HEADS + g + 1] for i in range(3)
    )
    return peak, high + low


def merge_kernel(keep_ref, came_ref, out_ref):
    peers, _, slots, _ = keep_ref.shape
    flat = (peers * slots, HEAD_SIZE)
    mine = keep_ref[:, KEY_VALUE_HEADS].reshape(flat)
    theirs = came_ref[:, KEY_VALUE_HEADS].astype(F32).reshape(flat)
    lane = lax.broadcasted_iota(jnp.int32, flat, 1)
    state = jnp.zeros(flat, F32)
    for g in range(KEY_VALUE_HEADS):
        my_peak, my_total = state_columns(mine, g)
        their_peak, their_total = state_columns(theirs, g)
        peak = jnp.maximum(my_peak, their_peak)
        my_scale, their_scale = jnp.exp(my_peak - peak), jnp.exp(their_peak - peak)
        total = my_total * my_scale + their_total * their_scale
        summed = (
            keep_ref[:, g].reshape(flat) * my_scale
            + came_ref[:, g].astype(F32).reshape(flat) * their_scale
        )
        total_high = rounded(total)
        for index, column in enumerate((peak, total_high, total - total_high)):
            state = jnp.where(lane == index * KEY_VALUE_HEADS + g, column, state)
        out_ref[:, g] = summed.astype(BF16).reshape(peers, slots, HEAD_SIZE)
    out_ref[:, KEY_VALUE_HEADS] = state.astype(BF16).reshape(peers, slots, HEAD_SIZE)


def merge(keep, came):
    return pl.pallas_call(
        merge_kernel,
        out_shape=pltpu.VMEM(came.shape, BF16),
        in_specs=[VMEM, VMEM],
        out_specs=VMEM,
        compiler_params=pltpu.CompilerParams(vmem_limit_bytes=8 * MIB),
        name="merge",
    )(in_vmem(keep), in_vmem(came))


def finish_kernel(parts_ref, gain_ref, out_ref, row_ref):
    peers, _, slots, _ = parts_ref.shape
    rows = slots // GROUP
    state = parts_ref[:, KEY_VALUE_HEADS].astype(F32)
    scale = jnp.exp(state - jnp.max(state, axis=0, keepdims=True))
    attended = []
    squares = jnp.zeros((slots, HEAD_SIZE), F32)
    for g in range(KEY_VALUE_HEADS):
        summed = jnp.zeros((slots, HEAD_SIZE), F32)
        total = jnp.zeros((slots, 1), F32)
        for peer in range(peers):
            by = scale[peer][:, g : g + 1]
            summed += parts_ref[peer, g].astype(F32) * by
            total += state_columns(state[peer], g)[1] * by
        one = rounded(summed / total)
        squares += one * one
        attended.append(one)
    mean_square = (
        jnp.sum(squares.reshape(rows, GROUP, HEAD_SIZE), axis=(1, 2), keepdims=True) / D + 1e-05
    )
    inverse = lax.rsqrt(mean_square)
    for g in range(KEY_VALUE_HEADS):
        normed = attended[g].reshape(rows, GROUP, HEAD_SIZE) * inverse * gain_ref[g][None]
        for row in range(rows):
            for head in range(GROUP):
                start = (g * GROUP + head) * HEAD_SIZE
                row_ref[row : row + 1, start : start + HEAD_SIZE] = normed[row, head : head + 1]
    packed = row_ref[...].astype(BF16)
    for peer in range(peers):
        out_ref[peer] = packed


def finish(parts, norm_gain):
    peers, _, slots, _ = parts.shape
    rows = slots // GROUP
    return pl.pallas_call(
        finish_kernel,
        out_shape=pltpu.VMEM((peers, rows, D), BF16),
        in_specs=[VMEM, VMEM],
        out_specs=VMEM,
        scratch_shapes=[pltpu.VMEM((rows, D), F32)],
        compiler_params=pltpu.CompilerParams(vmem_limit_bytes=8 * MIB),
        name="finish",
    )(in_vmem(parts), norm_gain.reshape(KEY_VALUE_HEADS, GROUP, HEAD_SIZE))


def feed_forward_kernel(
    near_ref, far_ref, gate_a_ref, gate_b_ref, up_hbm, down_hbm, keep_ref, send_ref,
    x_ref, up_ref, down_ref, up_sems, down_sems,
):
    half, width = near_ref.shape
    ups, downs = up_sems.shape[0], down_sems.shape[0]
    depth, step = up_ref.shape[0] // ups, width // downs
    up_parts = [pl.ds(i * depth, depth) for i in range(ups)]
    down_parts = [pl.ds(i * step, step) for i in range(downs)]
    up_copies = [
        pltpu.make_async_copy(up_hbm.at[part], up_ref.at[part], up_sems.at[i])
        for i, part in enumerate(up_parts)
    ]
    down_copies = [
        pltpu.make_async_copy(down_hbm.at[:, part], down_ref.at[:, part], down_sems.at[i])
        for i, part in enumerate(down_parts)
    ]

    up_copies[0].start()
    x_ref[:half] = near_ref[...]
    x_ref[half:] = far_ref[...]
    x = x_ref[...]

    def project(weight):
        return lax.dot_general(x, weight, ROWS_BY_ROWS, preferred_element_type=F32)

    gate_a = project(gate_a_ref[...])
    up_copies[1].start()
    gate = jnp.concatenate([gate_a, project(gate_b_ref[...])], axis=1)
    upward = []
    for i in range(ups):
        up_copies[i].wait()
        down_copies[i].start()
        upward.append(project(up_ref[i * depth : (i + 1) * depth]))
    upward = jnp.concatenate(upward, axis=1)
    activated = (gate / (1.0 + jnp.exp(-gate)) * upward).astype(BF16)
    for i in range(downs):
        if i + ups < downs:
            down_copies[i + ups].start()
        down_copies[i].wait()
        out = jnp.dot(activated, down_ref[:, down_parts[i]], preferred_element_type=F32)
        keep_ref[:, down_parts[i]] = out[:half]
        send_ref[:, down_parts[i]] = out[half:].astype(BF16)


def feed_forward(near, far, gate_a, gate_b, up, down):
    half, width = near.shape
    ups, downs = 2, 4
    return pl.pallas_call(
        feed_forward_kernel,
        out_shape=(pltpu.VMEM(near.shape, F32), pltpu.VMEM(near.shape, BF16)),
        in_specs=[VMEM] * 4 + [ANY, ANY],
        out_specs=(VMEM, VMEM),
        scratch_shapes=[
            pltpu.VMEM((2 * half, width), BF16),
            pltpu.VMEM(up.shape, up.dtype),
            pltpu.VMEM(down.shape, down.dtype),
            pltpu.SemaphoreType.DMA((ups,)),
            pltpu.SemaphoreType.DMA((downs,)),
        ],
        compiler_params=pltpu.CompilerParams(vmem_limit_bytes=36 * MIB),
        cost_estimate=pl.CostEstimate(
            flops=12 * half * up.size, bytes_accessed=4 * down.size, transcendentals=half * up.shape[0]
        ),
        name="feed_forward",
    )(*(in_vmem(x) for x in (near, far, gate_a, gate_b)), in_hbm(up), in_hbm(down))


def stacked(blocks):
    peers, rows, _ = blocks.shape
    out = None
    for i in range(peers):
        edges = ((i * rows, (peers - 1 - i) * rows, 0), (0, 0, 0))
        placed = lax.pad(blocks[i], jnp.array(-jnp.inf, blocks.dtype), edges)
        out = placed if out is None else jnp.maximum(out, placed)
    return out


def local(
    queries,
    cached_key_rows,
    cached_value_rows,
    cache_position,
    lengths,
    norm_gain,
    gate_weight,
    up_weight,
    down_weight,
):
    devices = lax.axis_size("ctx")
    peers = devices // 2
    rows = queries.shape[0]
    around = [*range(0, peers, 2), *reversed(range(1, peers, 2))]
    same_core = [[2 * i + core for i in around] for core in range(2)]
    partners = [(i, i ^ 1) for i in range(devices)]

    def exchange(x):
        return lax.all_to_all(x, "ctx", 0, 0, axis_index_groups=same_core, tiled=True)

    def swap(x):
        return lax.ppermute(x, "ctx", partners)

    near = exchange(pack(queries, lengths, peers))
    first_rows = gate_weight.shape[0] * 6 // 7
    late_keys, near = lax.optimization_barrier((cached_key_rows, near))
    far = swap(near)
    keys, values, position = load(
        (late_keys, 0), (cached_value_rows, 0), (cache_position.reshape(1, -1), 0)
    )
    keep, send, gate_a = attend(near, far, position, keys, values, gate_weight, first_rows)
    late_gate, send = lax.optimization_barrier((gate_weight, send))
    came = swap(send)
    (gate_b,) = load((late_gate, first_rows))
    parts = exchange(merge(keep, came))
    near = stacked(exchange(finish(parts, norm_gain)))
    keep, send = feed_forward(near, swap(near), gate_a, gate_b, up_weight, down_weight)
    shares = (keep + swap(send).astype(F32)).astype(BF16)
    shares = exchange(shares.reshape(peers, rows, D))
    return jnp.sum(shares.astype(F32), axis=0).astype(BF16)


def solution(mesh):
    placed = (
        P(("groups", "ctx"), None),
        P(("groups", "ctx"), None),
        P(("groups", "ctx"), None),
        P(("groups", "ctx")),
        P(("groups", "ctx")),
        P(),
        P("ctx", None),
        P("ctx", None),
        P("ctx", None),
    )
    return jax.shard_map(
        local, mesh=mesh, in_specs=placed, out_specs=P(("groups", "ctx"), None), check_vma=False
    )
```

```python
import functools
import math

import jax
import jax.numpy as jnp
from jax import lax
from jax.experimental import pallas as pl
from jax.experimental.pallas import tpu as pltpu
from jax.sharding import PartitionSpec as P

D = 8192
QUERY_HEADS = 64
KEY_VALUE_HEADS = 8
HEAD_SIZE = 128
GROUP = QUERY_HEADS // KEY_VALUE_HEADS
F32 = jnp.float32
BF16 = jnp.bfloat16
SCALE = HEAD_SIZE ** (-0.5) * math.log2(math.e)
DEAD = -1e30
ROWS_BY_ROWS = (((1,), (1,)), ((), ()))
VMEM = pl.BlockSpec(memory_space=pltpu.VMEM)
ANY = pl.BlockSpec(memory_space=pl.ANY)
MIB = 1 << 20


def in_vmem(x):
    return pltpu.with_memory_space_constraint(x, pltpu.VMEM)


def in_hbm(x):
    return pltpu.with_memory_space_constraint(x, pltpu.HBM)


def rounded(x):
    return x.astype(BF16).astype(F32)


def pack_kernel(lengths_hbm, q_hbm, out_ref, slab_ref, lengths_ref, q_ref, sems):
    rows = q_ref.shape[0]
    copies = (
        pltpu.make_async_copy(q_hbm, q_ref, sems.at[0]),
        pltpu.make_async_copy(lengths_hbm, lengths_ref, sems.at[1]),
    )
    for copy in copies:
        copy.start()
    for copy in copies:
        copy.wait()
    q = q_ref[...].astype(F32)
    lane = lax.broadcasted_iota(jnp.int32, (GROUP, HEAD_SIZE), 1)
    for row in range(rows):
        for head in range(QUERY_HEADS):
            slot = row * GROUP + head % GROUP
            slab_ref[head // GROUP, slot : slot + 1, :] = q[
                row : row + 1, head * HEAD_SIZE : (head + 1) * HEAD_SIZE
            ]
        length = lengths_ref[row]
        high, low = (length >> 8).astype(F32), (length & 255).astype(F32)
        slab_ref[KEY_VALUE_HEADS, row * GROUP : (row + 1) * GROUP, :] = jnp.where(
            lane == 0, high, jnp.where(lane == 1, low, 0.0)
        )
    packed = slab_ref[...].astype(BF16)
    for peer in range(out_ref.shape[0]):
        out_ref[peer] = packed


def pack(queries, lengths, peers):
    slots = queries.shape[0] * GROUP
    shape = (KEY_VALUE_HEADS + 1, slots, HEAD_SIZE)
    return pl.pallas_call(
        pack_kernel,
        out_shape=pltpu.VMEM((peers,) + shape, BF16),
        in_specs=[ANY, ANY],
        out_specs=VMEM,
        scratch_shapes=[
            pltpu.VMEM(shape, F32),
            pltpu.SMEM(lengths.shape, lengths.dtype),
            pltpu.VMEM(queries.shape, queries.dtype),
            pltpu.SemaphoreType.DMA((2,)),
        ],
        compiler_params=pltpu.CompilerParams(vmem_limit_bytes=4 * MIB),
        name="pack",
    )(in_hbm(lengths), in_hbm(queries))


def load_kernel(*refs, starts):
    count = len(starts)
    copies = [
        pltpu.make_async_copy(
            refs[i].at[pl.ds(start, refs[count + i].shape[0])], refs[count + i], refs[-1].at[i]
        )
        for i, start in enumerate(starts)
    ]
    for copy in copies:
        copy.start()
    for copy in copies:
        copy.wait()


def load(*entries):
    shapes = [((rows,) + a.shape[1:], a.dtype) for a, _, rows in entries]
    return pl.pallas_call(
        functools.partial(load_kernel, starts=tuple(start for _, start, _ in entries)),
        out_shape=tuple(pltpu.VMEM(*shape) for shape in shapes),
        in_specs=[ANY] * len(entries),
        out_specs=(VMEM,) * len(entries),
        scratch_shapes=[pltpu.SemaphoreType.DMA((len(entries),))],
        compiler_params=pltpu.CompilerParams(vmem_limit_bytes=MIB),
        cost_estimate=pl.CostEstimate(
            flops=0, bytes_accessed=sum(2 * rows * a.shape[1] for a, _, rows in entries), transcendentals=0
        ),
        name="load",
    )(*(in_hbm(a) for a, _, _ in entries))


def attend_kernel(q_ref, position_ref, k_ref, v_ref, out_ref):
    peers, _, slots, _ = q_ref.shape
    flat = (peers * slots, HEAD_SIZE)
    numbers = q_ref[:, KEY_VALUE_HEADS].reshape(flat).astype(F32)
    lengths = numbers[:, 0:1] * 256.0 + numbers[:, 1:2]
    bias = jnp.where(position_ref[...].astype(F32) < lengths, 0.0, DEAD)
    lane = lax.broadcasted_iota(jnp.int32, flat, 1)
    state = jnp.zeros(flat, F32)
    for g in range(KEY_VALUE_HEADS):
        columns = slice(g * HEAD_SIZE, (g + 1) * HEAD_SIZE)
        scores = lax.dot_general(
            q_ref[:, g].reshape(flat), k_ref[:, columns], ROWS_BY_ROWS, preferred_element_type=F32
        )
        scores = scores * SCALE + bias
        peak = rounded(jnp.maximum(jnp.max(scores, axis=1, keepdims=True), 0.1 * DEAD))
        weights = jnp.exp2(scores - peak)
        total = jnp.sum(weights, axis=1, keepdims=True)
        summed = jnp.dot(weights.astype(BF16), v_ref[:, columns], preferred_element_type=F32)
        total_high = rounded(total)
        for index, column in enumerate((peak, total_high, total - total_high)):
            state = jnp.where(lane == index * KEY_VALUE_HEADS + g, column, state)
        out_ref[:, g] = summed.astype(out_ref.dtype).reshape(peers, slots, HEAD_SIZE)
    out_ref[:, KEY_VALUE_HEADS] = state.astype(out_ref.dtype).reshape(peers, slots, HEAD_SIZE)


def attend(q, position, keys, values, dtype):
    cells = q.size // HEAD_SIZE * keys.shape[0]
    return pl.pallas_call(
        attend_kernel,
        out_shape=pltpu.VMEM(q.shape, dtype),
        in_specs=[VMEM] * 4,
        out_specs=VMEM,
        compiler_params=pltpu.CompilerParams(vmem_limit_bytes=8 * MIB + 16 * q.size),
        cost_estimate=pl.CostEstimate(
            flops=4 * cells * HEAD_SIZE, bytes_accessed=4 * keys.size, transcendentals=cells
        ),
        name="attend",
    )(*(in_vmem(x) for x in (q, position, keys, values)))


def joined(states):
    lane = lax.broadcasted_iota(jnp.int32, states[0].shape, 1)
    peak = functools.reduce(jnp.maximum, states)
    scales = [jnp.exp2(state - peak) for state in states]
    total = jnp.zeros_like(peak)
    for state, scale in zip(states, scales):
        high = jnp.where(lane < 2 * KEY_VALUE_HEADS, state, 0.0)
        low = pltpu.roll(state, HEAD_SIZE - KEY_VALUE_HEADS, 1)
        total += (high + low) * pltpu.roll(scale, KEY_VALUE_HEADS, 1)
    return lane, peak, scales, total


def combine_kernel(*refs, count, order):
    sources, targets = refs[:count], refs[count:]
    per_target = targets[0].shape[0]
    chip = lax.axis_index("ctx") // 2 if order is not None else 0
    for place in range(per_target * len(targets)):
        index = place if order is None else chip ^ (order[place] // 2)
        target = targets[place // per_target].at[place % per_target]
        states = [ref[index, KEY_VALUE_HEADS].astype(F32) for ref in sources]
        lane, peak, scales, total = joined(states)
        high = rounded(total)
        low = pltpu.roll(total - high, KEY_VALUE_HEADS, 1)
        state = jnp.where(
            lane < KEY_VALUE_HEADS,
            peak,
            jnp.where(
                lane < 2 * KEY_VALUE_HEADS, high, jnp.where(lane < 3 * KEY_VALUE_HEADS, low, 0.0)
            ),
        )
        target[KEY_VALUE_HEADS] = state.astype(BF16)
        for g in range(KEY_VALUE_HEADS):
            target[g] = sum(
                ref[index, g].astype(F32) * scale[:, g : g + 1]
                for ref, scale in zip(sources, scales)
            ).astype(BF16)


def combine(sources, pieces, order=None):
    blocks = sources[0].shape[0] // pieces
    return pl.pallas_call(
        functools.partial(combine_kernel, count=len(sources), order=order),
        out_shape=(pltpu.VMEM((blocks,) + sources[0].shape[1:], BF16),) * pieces,
        in_specs=[VMEM] * len(sources),
        out_specs=(VMEM,) * pieces,
        compiler_params=pltpu.CompilerParams(vmem_limit_bytes=4 * MIB),
        name="combine",
    )(*(in_vmem(x) for x in sources))


def finish_kernel(mine_ref, came_ref, gain_ref, out_ref, row_ref):
    blocks, _, slots, _ = mine_ref.shape
    rows = slots // GROUP
    for block in range(blocks):
        pair = (mine_ref.at[block], came_ref.at[blocks - 1 - block])
        _, _, scales, total = joined([ref[KEY_VALUE_HEADS].astype(F32) for ref in pair])
        attended = []
        squares = jnp.zeros((slots, HEAD_SIZE), F32)
        for g in range(KEY_VALUE_HEADS):
            summed = sum(
                ref[g].astype(F32) * scale[:, g : g + 1] for ref, scale in zip(pair, scales)
            )
            one = rounded(summed / total[:, KEY_VALUE_HEADS + g : KEY_VALUE_HEADS + g + 1])
            squares += one * one
            attended.append(one)
        mean_square = (
            jnp.sum(squares.reshape(rows, GROUP, HEAD_SIZE), axis=(1, 2), keepdims=True) / D + 1e-05
        )
        inverse = lax.rsqrt(mean_square)
        for g in range(KEY_VALUE_HEADS):
            normed = attended[g].reshape(rows, GROUP, HEAD_SIZE) * inverse * gain_ref[g][None]
            for row in range(rows):
                place = block * rows + row
                for head in range(GROUP):
                    start = (g * GROUP + head) * HEAD_SIZE
                    row_ref[place : place + 1, start : start + HEAD_SIZE] = normed[
                        row, head : head + 1
                    ]
    out_ref[...] = row_ref[...].astype(BF16)


def finish(mine, came, norm_gain):
    rows = mine.shape[0] * mine.shape[2] // GROUP
    return pl.pallas_call(
        finish_kernel,
        out_shape=pltpu.VMEM((rows, D), BF16),
        in_specs=[VMEM] * 3,
        out_specs=VMEM,
        scratch_shapes=[pltpu.VMEM((rows, D), F32)],
        compiler_params=pltpu.CompilerParams(vmem_limit_bytes=4 * MIB),
        name="finish",
    )(in_vmem(mine), in_vmem(came), norm_gain.reshape(KEY_VALUE_HEADS, GROUP, HEAD_SIZE))


def feed_forward_kernel(
    near_ref, far_ref, gate_a_ref, gate_b_ref, up_a_ref, up_hbm, down_hbm, keep_ref, send_ref,
    x_ref, up_b_ref, down_ref, up_sem, down_sems,
):
    half, width = near_ref.shape
    downs = down_sems.shape[0]
    step = width // downs
    parts = [pl.ds(i * step, step) for i in range(downs)]
    up_rows = up_b_ref.shape[0]
    up_copy = pltpu.make_async_copy(
        up_hbm.at[pl.ds(up_hbm.shape[0] - up_rows, up_rows)], up_b_ref, up_sem
    )
    down_copies = [
        pltpu.make_async_copy(down_hbm.at[:, part], down_ref.at[:, part], down_sems.at[i])
        for i, part in enumerate(parts)
    ]

    up_copy.start()
    x_ref[:half] = near_ref[...]
    x_ref[half:] = far_ref[...]
    x = x_ref[...]

    def project(weight_ref):
        return lax.dot_general(x, weight_ref[...], ROWS_BY_ROWS, preferred_element_type=F32)

    gate = [project(gate_a_ref)]
    down_copies[0].start()
    gate.append(project(gate_b_ref))
    gate = jnp.concatenate(gate, axis=1)
    gate = gate / (1.0 + jnp.exp(-gate))
    down_copies[1].start()
    upward = [project(up_a_ref)]
    up_copy.wait()
    down_copies[2].start()
    upward.append(project(up_b_ref))
    activated = (gate * jnp.concatenate(upward, axis=1)).astype(BF16)
    for i, part in enumerate(parts):
        if i + 3 < downs:
            down_copies[i + 3].start()
        down_copies[i].wait()
        out = jnp.dot(activated, down_ref[:, part], preferred_element_type=F32)
        keep_ref[:, part] = out[:half]
        send_ref[:, part] = out[half:].astype(BF16)


def feed_forward(near, far, gate_a, gate_b, up_a, up, down):
    half, width = near.shape
    downs = 4
    return pl.pallas_call(
        feed_forward_kernel,
        out_shape=(pltpu.VMEM(near.shape, F32), pltpu.VMEM(near.shape, BF16)),
        in_specs=[VMEM] * 5 + [ANY, ANY],
        out_specs=(VMEM, VMEM),
        scratch_shapes=[
            pltpu.VMEM((2 * half, width), BF16),
            pltpu.VMEM((up.shape[0] - up_a.shape[0], width), up.dtype),
            pltpu.VMEM(down.shape, down.dtype),
            pltpu.SemaphoreType.DMA,
            pltpu.SemaphoreType.DMA((downs,)),
        ],
        compiler_params=pltpu.CompilerParams(vmem_limit_bytes=28 * MIB),
        cost_estimate=pl.CostEstimate(
            flops=12 * half * up.size, bytes_accessed=3 * down.size, transcendentals=half * up.shape[0]
        ),
        name="feed_forward",
    )(*(in_vmem(x) for x in (near, far, gate_a, gate_b, up_a)), in_hbm(up), in_hbm(down))


def spread_kernel(keep_ref, came_ref, out_ref, *, masks):
    chip = lax.axis_index("ctx") // 2
    rows = out_ref.shape[1]
    for k, mask in enumerate(masks):
        part = slice(k * rows, (k + 1) * rows)
        share = keep_ref[part] + came_ref[part].astype(F32)
        out_ref[chip ^ (mask // 2)] = share.astype(BF16)


def spread(keep, came, masks):
    rows = keep.shape[0] // len(masks)
    return pl.pallas_call(
        functools.partial(spread_kernel, masks=masks),
        out_shape=pltpu.VMEM((len(masks), rows, keep.shape[1]), BF16),
        in_specs=[VMEM, VMEM],
        out_specs=VMEM,
        compiler_params=pltpu.CompilerParams(vmem_limit_bytes=4 * MIB),
        name="spread",
    )(in_vmem(keep), in_vmem(came))


def stacked(blocks):
    total, offset, out = sum(b.shape[0] for b in blocks), 0, None
    for block in blocks:
        rows = block.shape[0]
        edges = ((offset, total - offset - rows, 0), (0, 0, 0))
        placed = lax.pad(block, jnp.array(-jnp.inf, block.dtype), edges)
        out = placed if out is None else jnp.maximum(out, placed)
        offset += rows
    return out


def rounds_of(devices):
    rounds, bit, width = [], 2, 1
    while bit < devices:
        width = min(width, (devices // bit).bit_length() - 1)
        rounds.append([m * bit for m in range((1 << width) - 1, 0, -1)])
        bit, width = bit << width, 2
    return rounds


def order_of(rounds):
    masks = [0]
    for moves in rounds:
        masks = [mask ^ move for move in [0] + moves for mask in masks]
    return tuple(masks)


def trade(arrays, moves, devices, entry=None):
    if entry is not None:
        late, arrays = lax.optimization_barrier((entry[0], arrays))
    came = [
        lax.ppermute(array, "ctx", [(i, i ^ move) for i in range(devices)])
        for array, move in zip(arrays, moves)
    ]
    if entry is None:
        return came, None
    (part,) = load((late,) + entry[1:])
    return lax.optimization_barrier((came, part))


def local(
    queries,
    cached_key_rows,
    cached_value_rows,
    cache_position,
    lengths,
    norm_gain,
    gate_weight,
    up_weight,
    down_weight,
):
    devices = lax.axis_size("ctx")
    peers = devices // 2
    rows = queries.shape[0]
    same_core = [[2 * i + core for i in range(peers)] for core in range(2)]
    partners = [(i, i ^ 1) for i in range(devices)]

    def exchange(x):
        return lax.all_to_all(x, "ctx", 0, 0, axis_index_groups=same_core, tiled=True)

    def swap(x):
        return lax.ppermute(x, "ctx", partners)

    rounds = rounds_of(devices)
    order = order_of(rounds)
    hidden = gate_weight.shape[0]
    first = hidden // 2
    slots = cached_key_rows.shape[0]
    windows = [(gate_weight, 0, first), (gate_weight, first, hidden - first), (up_weight, 0, first)]
    loads = []

    near = exchange(pack(queries, lengths, peers))
    late_keys, near = lax.optimization_barrier((cached_key_rows, near))
    far = swap(near)
    keys, values, position = load(
        (late_keys, 0, slots), (cached_value_rows, 0, slots), (cache_position.reshape(1, -1), 0, 1)
    )
    send = attend(far, position, keys, values, BF16)
    late_near, send = lax.optimization_barrier((near, send))
    came = swap(send)
    keep = attend(late_near, position, keys, values, F32)

    parts = (keep, came)
    chips_order = order
    for number, moves in reversed(list(enumerate(rounds))[1:]):
        mine, *out = combine(parts, len(moves) + 1, chips_order)
        chips_order = None
        got, loaded = trade(out, moves, devices, windows[0] if not loads else None)
        loads += [] if loaded is None else [loaded]
        parts = (mine, *got)
    (mine,) = combine(parts, 1, chips_order)
    (came,), loaded = trade([mine], rounds[0], devices, windows[1])
    loads.append(loaded)
    block = finish(mine, came, norm_gain)
    for number, moves in enumerate(rounds[1:]):
        got, loaded = trade([block] * len(moves), moves, devices, windows[2] if number == 0 else None)
        loads += [] if loaded is None else [loaded]
        block = stacked([block, *got])
    keep, send = feed_forward(block, swap(block), *loads, up_weight, down_weight)
    shares = exchange(spread(keep, swap(send), order))
    return jnp.sum(shares.astype(F32), axis=0).astype(BF16)


def solution(mesh):
    placed = (
        P(("groups", "ctx"), None),
        P(("groups", "ctx"), None),
        P(("groups", "ctx"), None),
        P(("groups", "ctx")),
        P(("groups", "ctx")),
        P(),
        P("ctx", None),
        P("ctx", None),
        P("ctx", None),
    )
    return jax.shard_map(
        local, mesh=mesh, in_specs=placed, out_specs=P(("groups", "ctx"), None), check_vma=False
    )
```

```python
import functools
import math

import jax
import jax.numpy as jnp
from jax import lax
from jax.experimental import pallas as pl
from jax.experimental.pallas import tpu as pltpu
from jax.sharding import PartitionSpec as P

D = 8192
QUERY_HEADS = 64
KEY_VALUE_HEADS = 8
HEAD_SIZE = 128
GROUP = QUERY_HEADS // KEY_VALUE_HEADS
F32 = jnp.float32
BF16 = jnp.bfloat16
SCALE = HEAD_SIZE ** (-0.5) * math.log2(math.e)
DEAD = -1e30
ROWS_BY_ROWS = (((1,), (1,)), ((), ()))
VMEM = pl.BlockSpec(memory_space=pltpu.VMEM)
ANY = pl.BlockSpec(memory_space=pl.ANY)
MIB = 1 << 20


def in_vmem(x):
    return pltpu.with_memory_space_constraint(x, pltpu.VMEM)


def in_hbm(x):
    return pltpu.with_memory_space_constraint(x, pltpu.HBM)


def rounded(x):
    return x.astype(BF16).astype(F32)


def pack_kernel(lengths_hbm, q_hbm, out_ref, slab_ref, lengths_ref, q_ref, sems):
    rows = q_ref.shape[0]
    copies = (
        pltpu.make_async_copy(q_hbm, q_ref, sems.at[0]),
        pltpu.make_async_copy(lengths_hbm, lengths_ref, sems.at[1]),
    )
    for copy in copies:
        copy.start()
    for copy in copies:
        copy.wait()
    q = q_ref[...].astype(F32)
    lane = lax.broadcasted_iota(jnp.int32, (GROUP, HEAD_SIZE), 1)
    for row in range(rows):
        for head in range(QUERY_HEADS):
            slot = row * GROUP + head % GROUP
            slab_ref[head // GROUP, slot : slot + 1, :] = q[
                row : row + 1, head * HEAD_SIZE : (head + 1) * HEAD_SIZE
            ]
        length = lengths_ref[row]
        high, low = (length >> 8).astype(F32), (length & 255).astype(F32)
        slab_ref[KEY_VALUE_HEADS, row * GROUP : (row + 1) * GROUP, :] = jnp.where(
            lane == 0, high, jnp.where(lane == 1, low, 0.0)
        )
    packed = slab_ref[...].astype(BF16)
    for peer in range(out_ref.shape[0]):
        out_ref[peer] = packed


def pack(queries, lengths, peers):
    slots = queries.shape[0] * GROUP
    shape = (KEY_VALUE_HEADS + 1, slots, HEAD_SIZE)
    return pl.pallas_call(
        pack_kernel,
        out_shape=pltpu.VMEM((peers,) + shape, BF16),
        in_specs=[ANY, ANY],
        out_specs=VMEM,
        scratch_shapes=[
            pltpu.VMEM(shape, F32),
            pltpu.SMEM(lengths.shape, lengths.dtype),
            pltpu.VMEM(queries.shape, queries.dtype),
            pltpu.SemaphoreType.DMA((2,)),
        ],
        compiler_params=pltpu.CompilerParams(vmem_limit_bytes=4 * MIB),
        name="pack",
    )(in_hbm(lengths), in_hbm(queries))


def load_kernel(*refs, starts):
    count = len(starts)
    copies = [
        pltpu.make_async_copy(
            refs[i].at[pl.ds(start, refs[count + i].shape[0])], refs[count + i], refs[-1].at[i]
        )
        for i, start in enumerate(starts)
    ]
    for copy in copies:
        copy.start()
    for copy in copies:
        copy.wait()


def load(*entries):
    shapes = [((rows,) + a.shape[1:], a.dtype) for a, _, rows in entries]
    return pl.pallas_call(
        functools.partial(load_kernel, starts=tuple(start for _, start, _ in entries)),
        out_shape=tuple(pltpu.VMEM(*shape) for shape in shapes),
        in_specs=[ANY] * len(entries),
        out_specs=(VMEM,) * len(entries),
        scratch_shapes=[pltpu.SemaphoreType.DMA((len(entries),))],
        compiler_params=pltpu.CompilerParams(vmem_limit_bytes=MIB),
        cost_estimate=pl.CostEstimate(
            flops=0, bytes_accessed=sum(2 * rows * a.shape[1] for a, _, rows in entries), transcendentals=0
        ),
        name="load",
    )(*(in_hbm(a) for a, _, _ in entries))


def attend_kernel(q_ref, position_ref, k_ref, v_ref, out_ref):
    peers, _, slots, _ = q_ref.shape
    flat = (peers * slots, HEAD_SIZE)
    numbers = q_ref[:, KEY_VALUE_HEADS].reshape(flat).astype(F32)
    lengths = numbers[:, 0:1] * 256.0 + numbers[:, 1:2]
    bias = jnp.where(position_ref[...].astype(F32) < lengths, 0.0, DEAD)
    lane = lax.broadcasted_iota(jnp.int32, flat, 1)
    state = jnp.zeros(flat, F32)

    def columns(g):
        return slice(g * HEAD_SIZE, (g + 1) * HEAD_SIZE)

    def score(g):
        return lax.dot_general(
            q_ref[:, g].reshape(flat), k_ref[:, columns(g)], ROWS_BY_ROWS, preferred_element_type=F32
        )

    def add_up(g, weights):
        summed = jnp.dot(weights, v_ref[:, columns(g)], preferred_element_type=F32)
        out_ref[:, g] = summed.astype(out_ref.dtype).reshape(peers, slots, HEAD_SIZE)

    coming = score(0)
    waiting = None
    for g in range(KEY_VALUE_HEADS):
        scores = coming * SCALE + bias
        if g + 1 < KEY_VALUE_HEADS:
            coming = score(g + 1)
        peak = rounded(jnp.maximum(jnp.max(scores, axis=1, keepdims=True), 0.1 * DEAD))
        weights = jnp.exp2(scores - peak)
        total = jnp.sum(weights, axis=1, keepdims=True)
        if waiting is not None:
            add_up(g - 1, waiting)
        waiting = weights.astype(BF16)
        total_high = rounded(total)
        for index, column in enumerate((peak, total_high, total - total_high)):
            state = jnp.where(lane == index * KEY_VALUE_HEADS + g, column, state)
    add_up(KEY_VALUE_HEADS - 1, waiting)
    out_ref[:, KEY_VALUE_HEADS] = state.astype(out_ref.dtype).reshape(peers, slots, HEAD_SIZE)


def attend(q, position, keys, values, dtype):
    cells = q.size // HEAD_SIZE * keys.shape[0]
    return pl.pallas_call(
        attend_kernel,
        out_shape=pltpu.VMEM(q.shape, dtype),
        in_specs=[VMEM] * 4,
        out_specs=VMEM,
        compiler_params=pltpu.CompilerParams(vmem_limit_bytes=8 * MIB + 16 * q.size),
        cost_estimate=pl.CostEstimate(
            flops=4 * cells * HEAD_SIZE, bytes_accessed=4 * keys.size, transcendentals=cells
        ),
        name="attend",
    )(*(in_vmem(x) for x in (q, position, keys, values)))


def joined(states):
    lane = lax.broadcasted_iota(jnp.int32, states[0].shape, 1)
    peak = functools.reduce(jnp.maximum, states)
    scales = [jnp.exp2(state - peak) for state in states]
    total = jnp.zeros_like(peak)
    for state, scale in zip(states, scales):
        high = jnp.where(lane < 2 * KEY_VALUE_HEADS, state, 0.0)
        low = pltpu.roll(state, HEAD_SIZE - KEY_VALUE_HEADS, 1)
        total += (high + low) * pltpu.roll(scale, KEY_VALUE_HEADS, 1)
    return lane, peak, scales, total


def combine_kernel(*refs, count, order):
    sources, targets = refs[:count], refs[count:]
    per_target, _, slots, _ = targets[0].shape
    places = range(per_target * len(targets))
    chip = lax.axis_index("ctx") // 2 if order is not None else 0
    indices = [place if order is None else chip ^ (order[place] // 2) for place in places]
    lane, peak, scales, total = joined(
        [
            jnp.concatenate([ref[index, KEY_VALUE_HEADS].astype(F32) for index in indices], axis=0)
            for ref in sources
        ]
    )
    high = rounded(total)
    low = pltpu.roll(total - high, KEY_VALUE_HEADS, 1)
    state = jnp.where(
        lane < KEY_VALUE_HEADS,
        peak,
        jnp.where(lane < 2 * KEY_VALUE_HEADS, high, jnp.where(lane < 3 * KEY_VALUE_HEADS, low, 0.0)),
    ).astype(BF16)
    for place, index in zip(places, indices):
        target = targets[place // per_target].at[place % per_target]
        part = slice(place * slots, (place + 1) * slots)
        target[KEY_VALUE_HEADS] = state[part]
        for g in range(KEY_VALUE_HEADS):
            target[g] = sum(
                ref[index, g].astype(F32) * scale[part, g : g + 1]
                for ref, scale in zip(sources, scales)
            ).astype(BF16)


def combine(sources, pieces, order=None):
    blocks = sources[0].shape[0] // pieces
    return pl.pallas_call(
        functools.partial(combine_kernel, count=len(sources), order=order),
        out_shape=(pltpu.VMEM((blocks,) + sources[0].shape[1:], BF16),) * pieces,
        in_specs=[VMEM] * len(sources),
        out_specs=(VMEM,) * pieces,
        compiler_params=pltpu.CompilerParams(vmem_limit_bytes=4 * MIB),
        name="combine",
    )(*(in_vmem(x) for x in sources))


def finish_kernel(mine_ref, came_ref, gain_ref, out_ref, row_ref):
    blocks, _, slots, _ = mine_ref.shape
    rows = slots // GROUP
    for block in range(blocks):
        pair = (mine_ref.at[block], came_ref.at[blocks - 1 - block])
        _, _, scales, total = joined([ref[KEY_VALUE_HEADS].astype(F32) for ref in pair])
        attended = []
        squares = jnp.zeros((slots, HEAD_SIZE), F32)
        for g in range(KEY_VALUE_HEADS):
            summed = sum(
                ref[g].astype(F32) * scale[:, g : g + 1] for ref, scale in zip(pair, scales)
            )
            one = rounded(summed / total[:, KEY_VALUE_HEADS + g : KEY_VALUE_HEADS + g + 1])
            squares += one * one
            attended.append(one)
        mean_square = (
            jnp.sum(squares.reshape(rows, GROUP, HEAD_SIZE), axis=(1, 2), keepdims=True) / D + 1e-05
        )
        inverse = lax.rsqrt(mean_square)
        for g in range(KEY_VALUE_HEADS):
            normed = attended[g].reshape(rows, GROUP, HEAD_SIZE) * inverse * gain_ref[g][None]
            for row in range(rows):
                place = block * rows + row
                for head in range(GROUP):
                    start = (g * GROUP + head) * HEAD_SIZE
                    row_ref[place : place + 1, start : start + HEAD_SIZE] = normed[
                        row, head : head + 1
                    ]
    out_ref[...] = row_ref[...].astype(BF16)


def finish(mine, came, norm_gain):
    rows = mine.shape[0] * mine.shape[2] // GROUP
    return pl.pallas_call(
        finish_kernel,
        out_shape=pltpu.VMEM((rows, D), BF16),
        in_specs=[VMEM] * 3,
        out_specs=VMEM,
        scratch_shapes=[pltpu.VMEM((rows, D), F32)],
        compiler_params=pltpu.CompilerParams(vmem_limit_bytes=4 * MIB),
        name="finish",
    )(in_vmem(mine), in_vmem(came), norm_gain.reshape(KEY_VALUE_HEADS, GROUP, HEAD_SIZE))


def feed_forward_kernel(
    near_ref, far_ref, gate_a_ref, gate_b_ref, up_a_ref, up_hbm, down_hbm, keep_ref, send_ref,
    x_ref, up_b_ref, down_ref, up_sem, down_sems,
):
    half, width = near_ref.shape
    downs = down_sems.shape[0]
    step = width // downs
    parts = [pl.ds(i * step, step) for i in range(downs)]
    up_rows = up_b_ref.shape[0]
    up_copy = pltpu.make_async_copy(
        up_hbm.at[pl.ds(up_hbm.shape[0] - up_rows, up_rows)], up_b_ref, up_sem
    )
    down_copies = [
        pltpu.make_async_copy(down_hbm.at[:, part], down_ref.at[:, part], down_sems.at[i])
        for i, part in enumerate(parts)
    ]

    up_copy.start()
    x_ref[:half] = near_ref[...]
    x_ref[half:] = far_ref[...]
    x = x_ref[...]

    def project(weight_ref):
        return lax.dot_general(x, weight_ref[...], ROWS_BY_ROWS, preferred_element_type=F32)

    gate = [project(gate_a_ref)]
    down_copies[0].start()
    gate.append(project(gate_b_ref))
    gate = jnp.concatenate(gate, axis=1)
    gate = gate / (1.0 + jnp.exp(-gate))
    down_copies[1].start()
    upward = [project(up_a_ref)]
    up_copy.wait()
    down_copies[2].start()
    upward.append(project(up_b_ref))
    activated = (gate * jnp.concatenate(upward, axis=1)).astype(BF16)
    for i, part in enumerate(parts):
        if i + 3 < downs:
            down_copies[i + 3].start()
        down_copies[i].wait()
        out = jnp.dot(activated, down_ref[:, part], preferred_element_type=F32)
        keep_ref[:, part] = out[:half]
        send_ref[:, part] = out[half:].astype(BF16)


def feed_forward(near, far, gate_a, gate_b, up_a, up, down):
    half, width = near.shape
    downs = 4
    return pl.pallas_call(
        feed_forward_kernel,
        out_shape=(pltpu.VMEM(near.shape, F32), pltpu.VMEM(near.shape, BF16)),
        in_specs=[VMEM] * 5 + [ANY, ANY],
        out_specs=(VMEM, VMEM),
        scratch_shapes=[
            pltpu.VMEM((2 * half, width), BF16),
            pltpu.VMEM((up.shape[0] - up_a.shape[0], width), up.dtype),
            pltpu.VMEM(down.shape, down.dtype),
            pltpu.SemaphoreType.DMA,
            pltpu.SemaphoreType.DMA((downs,)),
        ],
        compiler_params=pltpu.CompilerParams(vmem_limit_bytes=28 * MIB),
        cost_estimate=pl.CostEstimate(
            flops=12 * half * up.size, bytes_accessed=3 * down.size, transcendentals=half * up.shape[0]
        ),
        name="feed_forward",
    )(*(in_vmem(x) for x in (near, far, gate_a, gate_b, up_a)), in_hbm(up), in_hbm(down))


def share_kernel(*refs, count):
    sources, targets = refs[:count], refs[count:]
    rows = targets[0].shape[0]
    total = sum(ref[...].astype(F32) for ref in sources)
    for i, target in enumerate(targets):
        target[...] = total[i * rows : (i + 1) * rows].astype(target.dtype)


def share(sources, pieces):
    rows, width = sources[0].shape
    shape = (rows // pieces, width)
    return pl.pallas_call(
        functools.partial(share_kernel, count=len(sources)),
        out_shape=(pltpu.VMEM(shape, F32),) + (pltpu.VMEM(shape, BF16),) * (pieces - 1),
        in_specs=[VMEM] * len(sources),
        out_specs=(VMEM,) * pieces,
        compiler_params=pltpu.CompilerParams(vmem_limit_bytes=8 * MIB),
        name="share",
    )(*(in_vmem(x) for x in sources))


def stacked(blocks):
    total, offset, out = sum(b.shape[0] for b in blocks), 0, None
    for block in blocks:
        rows = block.shape[0]
        edges = ((offset, total - offset - rows, 0), (0, 0, 0))
        placed = lax.pad(block, jnp.array(-jnp.inf, block.dtype), edges)
        out = placed if out is None else jnp.maximum(out, placed)
        offset += rows
    return out


def rounds_of(devices):
    rounds, bit, width = [], 2, 1
    while bit < devices:
        width = min(width, (devices // bit).bit_length() - 1)
        rounds.append([m * bit for m in ([2, 1, 3] if width == 2 else [1])])
        bit, width = bit << width, 2
    return rounds


def order_of(rounds):
    masks = [0]
    for moves in rounds:
        masks = [mask ^ move for move in [0] + moves for mask in masks]
    return tuple(masks)


def trade(arrays, moves, devices, entry=None):
    if entry is not None:
        late, arrays = lax.optimization_barrier((entry[0], arrays))
    came = [
        lax.ppermute(array, "ctx", [(i, i ^ move) for i in range(devices)])
        for array, move in zip(arrays, moves)
    ]
    if entry is None:
        return came, None
    (part,) = load((late,) + entry[1:])
    return lax.optimization_barrier((came, part))


def local(
    queries,
    cached_key_rows,
    cached_value_rows,
    cache_position,
    lengths,
    norm_gain,
    gate_weight,
    up_weight,
    down_weight,
):
    devices = lax.axis_size("ctx")
    peers = devices // 2
    rows = queries.shape[0]
    same_core = [[2 * i + core for i in range(peers)] for core in range(2)]
    partners = [(i, i ^ 1) for i in range(devices)]

    def exchange(x):
        return lax.all_to_all(x, "ctx", 0, 0, axis_index_groups=same_core, tiled=True)

    def swap(x):
        return lax.ppermute(x, "ctx", partners)

    rounds = rounds_of(devices)
    order = order_of(rounds)
    hidden = gate_weight.shape[0]
    first = hidden // 2
    slots = cached_key_rows.shape[0]
    windows = [(gate_weight, 0, first), (gate_weight, first, hidden - first), (up_weight, 0, first)]
    loads = []

    near = exchange(pack(queries, lengths, peers))
    late_keys, near = lax.optimization_barrier((cached_key_rows, near))
    far = swap(near)
    keys, values, position = load(
        (late_keys, 0, slots), (cached_value_rows, 0, slots), (cache_position.reshape(1, -1), 0, 1)
    )
    send = attend(far, position, keys, values, BF16)
    late_near, send = lax.optimization_barrier((near, send))
    came = swap(send)
    keep = attend(late_near, position, keys, values, F32)

    parts = (keep, came)
    chips_order = order
    for number, moves in reversed(list(enumerate(rounds))[1:]):
        mine, *out = combine(parts, len(moves) + 1, chips_order)
        chips_order = None
        got, loaded = trade(out, moves, devices, windows[0] if not loads else None)
        loads += [] if loaded is None else [loaded]
        parts = (mine, *got)
    (mine,) = combine(parts, 1, chips_order)
    (came,), loaded = trade([mine], rounds[0], devices, windows[1])
    loads.append(loaded)
    block = finish(mine, came, norm_gain)
    for number, moves in enumerate(rounds[1:]):
        got, loaded = trade([block] * len(moves), moves, devices, windows[2] if number == 0 else None)
        loads += [] if loaded is None else [loaded]
        block = stacked([block, *got])
    keep, send = feed_forward(block, swap(block), *loads, up_weight, down_weight)
    parts = (keep, swap(send))
    for moves in reversed(rounds):
        mine, *out = share(parts, len(moves) + 1)
        parts = (mine, *trade(out, moves, devices)[0])
    return sum(part.astype(F32) for part in parts).astype(BF16)


def solution(mesh):
    placed = (
        P(("groups", "ctx"), None),
        P(("groups", "ctx"), None),
        P(("groups", "ctx"), None),
        P(("groups", "ctx")),
        P(("groups", "ctx")),
        P(),
        P("ctx", None),
        P("ctx", None),
        P("ctx", None),
    )
    return jax.shard_map(
        local, mesh=mesh, in_specs=placed, out_specs=P(("groups", "ctx"), None), check_vma=False
    )
```

```python
import functools

import jax
import jax.numpy as jnp
from jax import lax
from jax.experimental import pallas as pl
from jax.experimental.pallas import tpu as pltpu
from jax.sharding import PartitionSpec as P

D = 8192
QUERY_HEADS = 64
KEY_VALUE_HEADS = 8
HEAD_SIZE = 128
GROUP = QUERY_HEADS // KEY_VALUE_HEADS
F32 = jnp.float32
BF16 = jnp.bfloat16
SCALE = HEAD_SIZE ** (-0.5)
DEAD = -1e30
ROWS_BY_ROWS = (((1,), (1,)), ((), ()))
VMEM = pl.BlockSpec(memory_space=pltpu.VMEM)
ANY = pl.BlockSpec(memory_space=pl.ANY)
MIB = 1 << 20


def in_vmem(x):
    return pltpu.with_memory_space_constraint(x, pltpu.VMEM)


def in_hbm(x):
    return pltpu.with_memory_space_constraint(x, pltpu.HBM)


def rounded(x):
    return x.astype(BF16).astype(F32)


def pack_kernel(lengths_hbm, q_hbm, out_ref, slab_ref, lengths_ref, q_ref, sems):
    rows = q_ref.shape[0]
    copies = (
        pltpu.make_async_copy(q_hbm, q_ref, sems.at[0]),
        pltpu.make_async_copy(lengths_hbm, lengths_ref, sems.at[1]),
    )
    for copy in copies:
        copy.start()
    for copy in copies:
        copy.wait()
    q = q_ref[...].astype(F32)
    lane = lax.broadcasted_iota(jnp.int32, (GROUP, HEAD_SIZE), 1)
    for row in range(rows):
        for head in range(QUERY_HEADS):
            slot = row * GROUP + head % GROUP
            slab_ref[head // GROUP, slot : slot + 1, :] = q[
                row : row + 1, head * HEAD_SIZE : (head + 1) * HEAD_SIZE
            ]
        length = lengths_ref[row]
        high, low = (length >> 8).astype(F32), (length & 255).astype(F32)
        slab_ref[KEY_VALUE_HEADS, row * GROUP : (row + 1) * GROUP, :] = jnp.where(
            lane == 0, high, jnp.where(lane == 1, low, 0.0)
        )
    packed = slab_ref[...].astype(BF16)
    for peer in range(out_ref.shape[0]):
        out_ref[peer] = packed


def pack(queries, lengths, peers):
    slots = queries.shape[0] * GROUP
    shape = (KEY_VALUE_HEADS + 1, slots, HEAD_SIZE)
    return pl.pallas_call(
        pack_kernel,
        out_shape=pltpu.VMEM((peers,) + shape, BF16),
        in_specs=[ANY, ANY],
        out_specs=VMEM,
        scratch_shapes=[
            pltpu.VMEM(shape, F32),
            pltpu.SMEM(lengths.shape, lengths.dtype),
            pltpu.VMEM(queries.shape, queries.dtype),
            pltpu.SemaphoreType.DMA((2,)),
        ],
        compiler_params=pltpu.CompilerParams(vmem_limit_bytes=4 * MIB),
        name="pack",
    )(in_hbm(lengths), in_hbm(queries))


def load_kernel(*refs, starts):
    count = len(starts)
    copies = [
        pltpu.make_async_copy(
            refs[i].at[pl.ds(start, refs[count + i].shape[0])], refs[count + i], refs[-1].at[i]
        )
        for i, start in enumerate(starts)
    ]
    for copy in copies:
        copy.start()
    for copy in copies:
        copy.wait()


def load(*entries):
    shapes = [((rows,) + a.shape[1:], a.dtype) for a, _, rows in entries]
    return pl.pallas_call(
        functools.partial(load_kernel, starts=tuple(start for _, start, _ in entries)),
        out_shape=tuple(pltpu.VMEM(*shape) for shape in shapes),
        in_specs=[ANY] * len(entries),
        out_specs=(VMEM,) * len(entries),
        scratch_shapes=[pltpu.SemaphoreType.DMA((len(entries),))],
        compiler_params=pltpu.CompilerParams(vmem_limit_bytes=MIB),
        cost_estimate=pl.CostEstimate(
            flops=0, bytes_accessed=sum(2 * rows * a.shape[1] for a, _, rows in entries), transcendentals=0
        ),
        name="load",
    )(*(in_hbm(a) for a, _, _ in entries))


def attend_kernel(q_ref, position_ref, k_ref, v_ref, out_ref):
    peers, _, slots, _ = q_ref.shape
    flat = (peers * slots, HEAD_SIZE)
    numbers = q_ref[:, KEY_VALUE_HEADS].reshape(flat).astype(F32)
    lengths = numbers[:, 0:1] * 256.0 + numbers[:, 1:2]
    bias = jnp.where(position_ref[...].astype(F32) < lengths, 0.0, DEAD)
    lane = lax.broadcasted_iota(jnp.int32, flat, 1)
    state = jnp.zeros(flat, F32)

    def columns(g):
        return slice(g * HEAD_SIZE, (g + 1) * HEAD_SIZE)

    def score(g):
        return lax.dot_general(
            q_ref[:, g].reshape(flat), k_ref[:, columns(g)], ROWS_BY_ROWS, preferred_element_type=F32
        )

    def add_up(g, weights):
        summed = jnp.dot(weights, v_ref[:, columns(g)], preferred_element_type=F32)
        out_ref[:, g] = summed.astype(out_ref.dtype).reshape(peers, slots, HEAD_SIZE)

    coming = score(0)
    waiting = None
    for g in range(KEY_VALUE_HEADS):
        scores = coming * SCALE + bias
        if g + 1 < KEY_VALUE_HEADS:
            coming = score(g + 1)
        peak = rounded(jnp.maximum(jnp.max(scores, axis=1, keepdims=True), 0.1 * DEAD))
        weights = jnp.exp(scores - peak)
        total = jnp.sum(weights, axis=1, keepdims=True)
        if waiting is not None:
            add_up(g - 1, waiting)
        waiting = weights.astype(BF16)
        total_high = rounded(total)
        for index, column in enumerate((peak, total_high, total - total_high)):
            state = jnp.where(lane == index * KEY_VALUE_HEADS + g, column, state)
    add_up(KEY_VALUE_HEADS - 1, waiting)
    out_ref[:, KEY_VALUE_HEADS] = state.astype(out_ref.dtype).reshape(peers, slots, HEAD_SIZE)


def attend(q, position, keys, values, dtype):
    cells = q.size // HEAD_SIZE * keys.shape[0]
    return pl.pallas_call(
        attend_kernel,
        out_shape=pltpu.VMEM(q.shape, dtype),
        in_specs=[VMEM] * 4,
        out_specs=VMEM,
        compiler_params=pltpu.CompilerParams(vmem_limit_bytes=8 * MIB + 16 * q.size),
        cost_estimate=pl.CostEstimate(
            flops=4 * cells * HEAD_SIZE, bytes_accessed=4 * keys.size, transcendentals=cells
        ),
        name="attend",
    )(*(in_vmem(x) for x in (q, position, keys, values)))


def joined(states):
    lane = lax.broadcasted_iota(jnp.int32, states[0].shape, 1)
    peak = functools.reduce(jnp.maximum, states)
    scales = [jnp.exp(state - peak) for state in states]
    total = jnp.zeros_like(peak)
    for state, scale in zip(states, scales):
        high = jnp.where(lane < 2 * KEY_VALUE_HEADS, state, 0.0)
        low = pltpu.roll(state, HEAD_SIZE - KEY_VALUE_HEADS, 1)
        total += (high + low) * pltpu.roll(scale, KEY_VALUE_HEADS, 1)
    return lane, peak, scales, total


def combine_kernel(*refs, count, order):
    sources, targets = refs[:count], refs[count:]
    per_target, _, slots, _ = targets[0].shape
    places = range(per_target * len(targets))
    chip = lax.axis_index("ctx") // 2 if order is not None else 0
    indices = [place if order is None else chip ^ (order[place] // 2) for place in places]
    lane, peak, scales, total = joined(
        [
            jnp.concatenate([ref[index, KEY_VALUE_HEADS].astype(F32) for index in indices], axis=0)
            for ref in sources
        ]
    )
    high = rounded(total)
    low = pltpu.roll(total - high, KEY_VALUE_HEADS, 1)
    state = jnp.where(
        lane < KEY_VALUE_HEADS,
        peak,
        jnp.where(lane < 2 * KEY_VALUE_HEADS, high, jnp.where(lane < 3 * KEY_VALUE_HEADS, low, 0.0)),
    ).astype(BF16)
    for place, index in zip(places, indices):
        target = targets[place // per_target].at[place % per_target]
        part = slice(place * slots, (place + 1) * slots)
        target[KEY_VALUE_HEADS] = state[part]
        for g in range(KEY_VALUE_HEADS):
            target[g] = sum(
                ref[index, g].astype(F32) * scale[part, g : g + 1]
                for ref, scale in zip(sources, scales)
            ).astype(BF16)


def combine(sources, pieces, order=None):
    blocks = sources[0].shape[0] // pieces
    return pl.pallas_call(
        functools.partial(combine_kernel, count=len(sources), order=order),
        out_shape=(pltpu.VMEM((blocks,) + sources[0].shape[1:], BF16),) * pieces,
        in_specs=[VMEM] * len(sources),
        out_specs=(VMEM,) * pieces,
        compiler_params=pltpu.CompilerParams(vmem_limit_bytes=4 * MIB),
        name="combine",
    )(*(in_vmem(x) for x in sources))


def finish_kernel(mine_ref, came_ref, gain_ref, out_ref, row_ref):
    blocks, _, slots, _ = mine_ref.shape
    rows = slots // GROUP
    for block in range(blocks):
        pair = (mine_ref.at[block], came_ref.at[blocks - 1 - block])
        _, _, scales, total = joined([ref[KEY_VALUE_HEADS].astype(F32) for ref in pair])
        attended = []
        squares = jnp.zeros((slots, HEAD_SIZE), F32)
        for g in range(KEY_VALUE_HEADS):
            summed = sum(
                ref[g].astype(F32) * scale[:, g : g + 1] for ref, scale in zip(pair, scales)
            )
            one = rounded(summed / total[:, KEY_VALUE_HEADS + g : KEY_VALUE_HEADS + g + 1])
            squares += one * one
            attended.append(one)
        mean_square = (
            jnp.sum(squares.reshape(rows, GROUP, HEAD_SIZE), axis=(1, 2), keepdims=True) / D + 1e-05
        )
        inverse = lax.rsqrt(mean_square)
        for g in range(KEY_VALUE_HEADS):
            normed = attended[g].reshape(rows, GROUP, HEAD_SIZE) * inverse * gain_ref[g][None]
            for row in range(rows):
                place = block * rows + row
                for head in range(GROUP):
                    start = (g * GROUP + head) * HEAD_SIZE
                    row_ref[place : place + 1, start : start + HEAD_SIZE] = normed[
                        row, head : head + 1
                    ]
    out_ref[...] = row_ref[...].astype(BF16)


def finish(mine, came, norm_gain):
    rows = mine.shape[0] * mine.shape[2] // GROUP
    return pl.pallas_call(
        finish_kernel,
        out_shape=pltpu.VMEM((rows, D), BF16),
        in_specs=[VMEM] * 3,
        out_specs=VMEM,
        scratch_shapes=[pltpu.VMEM((rows, D), F32)],
        compiler_params=pltpu.CompilerParams(vmem_limit_bytes=4 * MIB),
        name="finish",
    )(in_vmem(mine), in_vmem(came), norm_gain.reshape(KEY_VALUE_HEADS, GROUP, HEAD_SIZE))


def feed_forward_kernel(
    near_ref, far_ref, gate_a_ref, gate_b_ref, up_a_ref, up_hbm, down_hbm, keep_ref, send_ref,
    x_ref, up_b_ref, down_ref, up_sem, down_sems,
):
    half, width = near_ref.shape
    downs = down_sems.shape[0]
    step = width // downs
    parts = [pl.ds(i * step, step) for i in range(downs)]
    up_rows = up_b_ref.shape[0]
    up_copy = pltpu.make_async_copy(
        up_hbm.at[pl.ds(up_hbm.shape[0] - up_rows, up_rows)], up_b_ref, up_sem
    )
    down_copies = [
        pltpu.make_async_copy(down_hbm.at[:, part], down_ref.at[:, part], down_sems.at[i])
        for i, part in enumerate(parts)
    ]

    up_copy.start()
    x_ref[:half] = near_ref[...]
    x_ref[half:] = far_ref[...]
    x = x_ref[...]

    def project(weight_ref):
        return lax.dot_general(x, weight_ref[...], ROWS_BY_ROWS, preferred_element_type=F32)

    gate = [project(gate_a_ref)]
    down_copies[0].start()
    gate.append(project(gate_b_ref))
    gate = jnp.concatenate(gate, axis=1)
    gate = gate / (1.0 + jnp.exp(-gate))
    down_copies[1].start()
    upward = [project(up_a_ref)]
    up_copy.wait()
    down_copies[2].start()
    upward.append(project(up_b_ref))
    activated = (gate * jnp.concatenate(upward, axis=1)).astype(BF16)
    for i, part in enumerate(parts):
        if i + 3 < downs:
            down_copies[i + 3].start()
        down_copies[i].wait()
        out = jnp.dot(activated, down_ref[:, part], preferred_element_type=F32)
        keep_ref[:, part] = out[:half]
        send_ref[:, part] = out[half:].astype(BF16)


def feed_forward(near, far, gate_a, gate_b, up_a, up, down):
    half, width = near.shape
    downs = 4
    return pl.pallas_call(
        feed_forward_kernel,
        out_shape=(pltpu.VMEM(near.shape, F32), pltpu.VMEM(near.shape, BF16)),
        in_specs=[VMEM] * 5 + [ANY, ANY],
        out_specs=(VMEM, VMEM),
        scratch_shapes=[
            pltpu.VMEM((2 * half, width), BF16),
            pltpu.VMEM((up.shape[0] - up_a.shape[0], width), up.dtype),
            pltpu.VMEM(down.shape, down.dtype),
            pltpu.SemaphoreType.DMA,
            pltpu.SemaphoreType.DMA((downs,)),
        ],
        compiler_params=pltpu.CompilerParams(vmem_limit_bytes=28 * MIB),
        cost_estimate=pl.CostEstimate(
            flops=12 * half * up.size, bytes_accessed=3 * down.size, transcendentals=half * up.shape[0]
        ),
        name="feed_forward",
    )(*(in_vmem(x) for x in (near, far, gate_a, gate_b, up_a)), in_hbm(up), in_hbm(down))


def share_kernel(*refs, count):
    sources, targets = refs[:count], refs[count:]
    rows = targets[0].shape[0]
    total = sum(ref[...].astype(F32) for ref in sources)
    for i, target in enumerate(targets):
        target[...] = total[i * rows : (i + 1) * rows].astype(target.dtype)


def share(sources, pieces):
    rows, width = sources[0].shape
    shape = (rows // pieces, width)
    return pl.pallas_call(
        functools.partial(share_kernel, count=len(sources)),
        out_shape=(pltpu.VMEM(shape, F32),) + (pltpu.VMEM(shape, BF16),) * (pieces - 1),
        in_specs=[VMEM] * len(sources),
        out_specs=(VMEM,) * pieces,
        compiler_params=pltpu.CompilerParams(vmem_limit_bytes=8 * MIB),
        name="share",
    )(*(in_vmem(x) for x in sources))


def stacked(blocks):
    total, offset, out = sum(b.shape[0] for b in blocks), 0, None
    for block in blocks:
        rows = block.shape[0]
        edges = ((offset, total - offset - rows, 0), (0, 0, 0))
        placed = lax.pad(block, jnp.array(-jnp.inf, block.dtype), edges)
        out = placed if out is None else jnp.maximum(out, placed)
        offset += rows
    return out


def rounds_of(devices):
    rounds, bit, width = [], 2, 1
    while bit < devices:
        width = min(width, (devices // bit).bit_length() - 1)
        rounds.append([m * bit for m in ([2, 1, 3] if width == 2 else [1])])
        bit, width = bit << width, 2
    return rounds


def order_of(rounds):
    masks = [0]
    for moves in rounds:
        masks = [mask ^ move for move in [0] + moves for mask in masks]
    return tuple(masks)


def trade(arrays, moves, devices, entry=None):
    if entry is not None:
        late, arrays = lax.optimization_barrier((entry[0], arrays))
    came = [
        lax.ppermute(array, "ctx", [(i, i ^ move) for i in range(devices)])
        for array, move in zip(arrays, moves)
    ]
    if entry is None:
        return came, None
    (part,) = load((late,) + entry[1:])
    return lax.optimization_barrier((came, part))


def local(
    queries,
    cached_key_rows,
    cached_value_rows,
    cache_position,
    lengths,
    norm_gain,
    gate_weight,
    up_weight,
    down_weight,
):
    devices = lax.axis_size("ctx")
    peers = devices // 2
    rows = queries.shape[0]
    same_core = [[2 * i + core for i in range(peers)] for core in range(2)]
    partners = [(i, i ^ 1) for i in range(devices)]

    def exchange(x):
        return lax.all_to_all(x, "ctx", 0, 0, axis_index_groups=same_core, tiled=True)

    def swap(x):
        return lax.ppermute(x, "ctx", partners)

    rounds = rounds_of(devices)
    order = order_of(rounds)
    hidden = gate_weight.shape[0]
    first = hidden // 2
    slots = cached_key_rows.shape[0]
    windows = [(gate_weight, 0, first), (gate_weight, first, hidden - first), (up_weight, 0, first)]
    loads = []

    near = exchange(pack(queries, lengths, peers))
    late_keys, near = lax.optimization_barrier((cached_key_rows, near))
    far = swap(near)
    keys, values, position = load(
        (late_keys, 0, slots), (cached_value_rows, 0, slots), (cache_position.reshape(1, -1), 0, 1)
    )
    send = attend(far, position, keys, values, BF16)
    late_near, send = lax.optimization_barrier((near, send))
    came = swap(send)
    keep = attend(late_near, position, keys, values, F32)

    parts = (keep, came)
    chips_order = order
    for number, moves in reversed(list(enumerate(rounds))[1:]):
        mine, *out = combine(parts, len(moves) + 1, chips_order)
        chips_order = None
        got, loaded = trade(out, moves, devices, windows[0] if not loads else None)
        loads += [] if loaded is None else [loaded]
        parts = (mine, *got)
    (mine,) = combine(parts, 1, chips_order)
    (came,), loaded = trade([mine], rounds[0], devices, windows[1])
    loads.append(loaded)
    block = finish(mine, came, norm_gain)
    for number, moves in enumerate(rounds[1:]):
        got, loaded = trade([block] * len(moves), moves, devices, windows[2] if number == 0 else None)
        loads += [] if loaded is None else [loaded]
        block = stacked([block, *got])
    keep, send = feed_forward(block, swap(block), *loads, up_weight, down_weight)
    parts = (keep, swap(send))
    for moves in reversed(rounds):
        mine, *out = share(parts, len(moves) + 1)
        parts = (mine, *trade(out, moves, devices)[0])
    return sum(part.astype(F32) for part in parts).astype(BF16)


def solution(mesh):
    placed = (
        P(("groups", "ctx"), None),
        P(("groups", "ctx"), None),
        P(("groups", "ctx"), None),
        P(("groups", "ctx")),
        P(("groups", "ctx")),
        P(),
        P("ctx", None),
        P("ctx", None),
        P("ctx", None),
    )
    return jax.shard_map(
        local, mesh=mesh, in_specs=placed, out_specs=P(("groups", "ctx"), None), check_vma=False
    )
```
